32 devices in a mesh: leaf: 16 (over z, y, x), cols: 2 (over core).
Axes of the slice: x: 2, y: 2, z: 4, core: 2. Of those that a mesh axis runs over, the one named last changes fastest.
Arguments:
- left_panels: bfloat16 [4096, 28672], P('cols', 'leaf'), may hold values from -0.125 to 0.125
- right_panels: bfloat16 [4096, 28672], P('cols', 'leaf'), may hold values from -6 to 6
- col_basis: bfloat16 [4096, 256], P('cols'), may hold values from -0.09375 to 0.09375
- row_bases: bfloat16 [4096, 2048], P('cols', 'leaf'), may hold values from -0.09375 to 0.09375
- old_cores: float32 [16, 256, 128], P('leaf'), may hold values from -6 to 6
- transfers: float32 [4, 2, 128, 128], replicated, may hold values from -0.375 to 0.375
- targets: int32 [448, 1], P('leaf'), may hold values from 0 to 15, as said below
Outputs:
- leaf_cores: float32 [16, 256, 128], P('leaf', 'cols')
- root_core: float32 [256, 128], P('cols', 'leaf')
The draws below stay inside these ranges and needn't reach their ends.
Inputs may be any that keep to these rules, and one draw needn't show every extreme that they name: `targets`: among the 28 panels of one index of leaf, every target block is named at most 2 times; one target block, the same for every index of leaf, is named exactly 2 times by every index.
All inputs are finite; a program needn't handle non-finite values.
Results may differ from the reference program's by a relative error of at most 0.002.
Values may be sent and summed in bfloat16 or wider, within the bound.
A program may use at most 128 MiB of HBM per device.

```python
import jax
import jax.numpy as jnp
from jax import lax

B = 4096
R = 64
KR = 128
KC = 256
CAP = 2
P_SIZE = 28
NP = 448
LEVELS = 4
N_LEAF = 16


def draw_targets(key, part):
    base_key = jax.random.fold_in(key, 11)
    hottest_key, pick_key, mix_key = jax.random.split(base_key, 3)
    hottest = jax.random.randint(hottest_key, (), 0, N_LEAF, dtype=jnp.int32)
    others = (hottest + 1 + jnp.arange((N_LEAF - 1) * CAP, dtype=jnp.int32) // CAP) % N_LEAF
    pick_keys = jax.random.split(pick_key, N_LEAF)
    mix_keys = jax.random.split(mix_key, N_LEAF)

    def one_block(pick_one, mix_one):
        chosen = jax.random.permutation(pick_one, others)[:P_SIZE - CAP]
        block_rows = jnp.concatenate([hottest + jnp.zeros((CAP,), jnp.int32), chosen])
        return jax.random.permutation(mix_one, block_rows)
    all_rows = jax.vmap(one_block)(pick_keys, mix_keys)
    return all_rows.reshape(N_LEAF * P_SIZE, 1).astype(jnp.int32)


def block_scale(own_key, extent, pieces, smallest, largest):
    level, own = 1.0, jax.random.fold_in(own_key, 6)
    for dim, parts in pieces:
        draws = jnp.exp(jax.random.uniform(jax.random.fold_in(own, dim), (parts,), jnp.float32, smallest / len(pieces), largest / len(pieces)))
        level = level * jnp.repeat(draws, extent[dim] // parts).reshape([-1 if axis == dim else 1 for axis in range(len(extent))])
    return level


def centred(own_key, extent, deviation, limit, pieces=(), kind=jnp.bfloat16):
    entries = jax.random.normal(own_key, extent, jnp.float32) * deviation
    if len(pieces) > 0:
        entries = block_scale(own_key, extent, pieces, -0.22, 0.18) * entries
    return jnp.clip(entries, min=-limit, max=limit).astype(kind)


def setup_inputs(seed: int = 0) -> dict:
    splits = jax.random.split(jax.random.key(seed), 8)
    left_panels = centred(splits[0], (B, NP * R), (P_SIZE * R) ** -0.5, 0.125, ((0, 2), (1, 16)))
    right_panels = centred(splits[1], (B, NP * R), 1.0, 6.0, ((0, 2), (1, 16)))
    col_basis = centred(splits[2], (B, KC), B ** -0.5, 0.09375, ((0, 2),))
    row_bases = centred(splits[3], (B, N_LEAF * KR), B ** -0.5, 0.09375, ((0, 2), (1, 16)))
    old_cores = centred(splits[4], (N_LEAF, KC, KR), 1.0, 6.0, ((0, 16),), jnp.float32)
    transfers = centred(splits[5], (LEVELS, 2, KR, KR), (2 * KR) ** -0.5, 0.375, (), jnp.float32)
    targets = draw_targets(jax.random.fold_in(splits[7], 71), 0)
    return dict(left_panels=left_panels, right_panels=right_panels, col_basis=col_basis, row_bases=row_bases, old_cores=old_cores, transfers=transfers, targets=targets)


def reference(left_panels, right_panels, col_basis, row_bases, old_cores, transfers, targets):
    coefficients = jnp.dot(col_basis.T, right_panels, preferred_element_type=jnp.float32).astype(jnp.bfloat16)
    owners = targets[:, 0].astype(jnp.int32)

    def add_panel(totals, panel_index):
        start = (panel_index * R).astype(jnp.int32)
        left_cols = lax.dynamic_slice_in_dim(left_panels, start, R, 1)
        coef_cols = lax.dynamic_slice_in_dim(coefficients, start, R, 1)
        product = jnp.dot(left_cols, coef_cols.T, preferred_element_type=jnp.float32)
        return totals.at[owners[panel_index]].add(product), None

    totals = jnp.zeros((N_LEAF, B, KC), jnp.float32)
    totals, _ = lax.scan(add_panel, totals, jnp.arange(NP, dtype=jnp.int32))
    row_basis = row_bases.astype(jnp.float32).reshape(B, N_LEAF, KR)
    projected = jnp.einsum("tbk,btr->tkr", totals, row_basis, precision=lax.Precision.HIGHEST)
    leaf_cores = old_cores + projected
    current = leaf_cores
    for depth_index in range(LEVELS):
        sibling_pairs = current.reshape(-1, 2, KC, KR)
        current = jnp.einsum("nkr,rs->nks", sibling_pairs[:, 0], transfers[depth_index, 0], precision=lax.Precision.HIGHEST) + jnp.einsum("nkr,rs->nks", sibling_pairs[:, 1], transfers[depth_index, 1], precision=lax.Precision.HIGHEST)
    return leaf_cores, current[0]
```

```python
import functools

import jax
import jax.numpy as jnp
from jax import lax
from jax.experimental import pallas as pl
from jax.experimental.pallas import tpu as pltpu
from jax.sharding import PartitionSpec as P

HIGHEST = lax.Precision.HIGHEST


def project_kernel(panel_rank, targets_ref, left_ref, bases_ref, out_ref):
    pair = 128 // panel_rank
    width = left_ref.shape[1]

    @pl.loop(0, width // 128)
    def _(step):
        start = pl.multiple_of(step * 128, 128)
        block = left_ref[:, pl.ds(start, 128)]
        for piece in range(pair):
            owner = targets_ref[step * pair + piece]
            whole = lax.dot_general(
                block,
                bases_ref[owner],
                (((0,), (0,)), ((), ())),
                preferred_element_type=jnp.float32,
            )
            rows = pl.ds(pl.multiple_of(start + piece * panel_rank, panel_rank), panel_rank)
            out_ref[rows, :] = whole[piece * panel_rank : (piece + 1) * panel_rank]


def project(targets, left, bases, panel_rank):
    return pl.pallas_call(
        functools.partial(project_kernel, panel_rank),
        out_shape=jax.ShapeDtypeStruct((left.shape[1], bases.shape[2]), jnp.float32),
        in_specs=[
            pl.BlockSpec(memory_space=pltpu.SMEM),
            pl.BlockSpec(memory_space=pltpu.VMEM),
            pl.BlockSpec(memory_space=pltpu.VMEM),
        ],
        out_specs=pl.BlockSpec(memory_space=pltpu.VMEM),
        compiler_params=pltpu.CompilerParams(vmem_limit_bytes=48 << 20),
    )(targets, left, bases)


def path_products(transfers):
    levels = transfers.shape[0]
    products = transfers[levels - 1]
    for level in range(levels - 2, -1, -1):
        products = jnp.einsum(
            "brs,nsk->nbrk", transfers[level], products, precision=HIGHEST
        ).reshape(-1, *transfers.shape[2:])
    return products


def split_dot(coef, value):
    high = value.astype(jnp.bfloat16)
    low = (value - high.astype(jnp.float32)).astype(jnp.bfloat16)
    return jnp.dot(coef, high, preferred_element_type=jnp.float32) + jnp.dot(
        coef, low, preferred_element_type=jnp.float32
    )


def local(left_panels, right_panels, col_basis, row_bases, old_cores, transfers, targets):
    n_leaf = lax.axis_size("leaf")
    n_cols = lax.axis_size("cols")
    panels = targets.shape[0]
    panel_rank = left_panels.shape[1] // panels
    rank = row_bases.shape[1]
    col_rank = col_basis.shape[1]
    share = col_rank // n_cols
    owners = targets[:, 0]

    bases = lax.all_gather(row_bases, "leaf", axis=0)
    partial_value = jnp.einsum(
        "bk,bn->kn", col_basis, right_panels, preferred_element_type=jnp.float32
    )
    coef = lax.psum_scatter(
        partial_value, "cols", scatter_dimension=0, tiled=True
    ).astype(jnp.bfloat16)
    paths = path_products(transfers)
    projected = lax.psum(project(owners, left_panels, bases, panel_rank), "cols")
    spread_owner = jnp.repeat(owners, panel_rank)
    mask = spread_owner[:, None] == jnp.arange(n_leaf, dtype=jnp.int32)[None, :]
    spread = jnp.where(mask[:, :, None], projected[:, None, :], 0.0)
    parts = split_dot(coef, spread.reshape(-1, n_leaf * rank))

    old_share = lax.dynamic_slice_in_dim(old_cores[0], lax.axis_index("cols") * share, share, 0)
    own_path = lax.dynamic_index_in_dim(paths, lax.axis_index("leaf"), 0, keepdims=False)
    root_part = jnp.dot(
        parts, paths.reshape(n_leaf * rank, rank), precision=HIGHEST
    ) + jnp.dot(old_share, own_path, precision=HIGHEST)
    strip = rank // n_leaf
    message = jnp.concatenate(
        [
            parts.reshape(share, n_leaf, rank),
            root_part.reshape(share, n_leaf, strip),
        ],
        axis=2,
    ).transpose(1, 0, 2)
    summed = lax.psum_scatter(message, "leaf", scatter_dimension=0, tiled=True)[0]
    leaf = summed[:, :rank] + old_share
    return leaf[None], summed[:, rank:]


def solution(mesh):
    placed = (
        P("cols", "leaf"),
        P("cols", "leaf"),
        P("cols", None),
        P("cols", "leaf"),
        P("leaf", None, None),
        P(),
        P("leaf", None),
    )
    return jax.shard_map(
        local,
        mesh=mesh,
        in_specs=placed,
        out_specs=(P("leaf", "cols", None), P("cols", "leaf")),
        check_vma=False,
    )
```

```python
import functools

import jax
import jax.numpy as jnp
from jax import lax
from jax.experimental import pallas as pl
from jax.experimental.pallas import tpu as pltpu
from jax.sharding import PartitionSpec as P

CAP = 2
HIGHEST = lax.Precision.HIGHEST
MESH = pl.DeviceIdType.MESH
CHUNK = 256


def dot_t(lhs, rhs):
    return lax.dot_general(
        lhs, rhs, (((0,), (0,)), ((), ())), preferred_element_type=jnp.float32
    )


def kernel(
    n, n_cols, panel_rank,
    source_ref, pair_ref, weight_ref, left_hbm, right_hbm, basis_ref, rows_hbm, old_ref, transfers_ref,
    leaf_ref, root_ref,
    left, right, bases, coefp, coefr, coeft, cores, coresr, paths, parts, partsr, strips, stripsr,
    load_sem, hop_send, hop_recv, coef_send, coef_recv, core_send, core_recv,
    part_send, part_recv, strip_send, strip_recv,
):
    me = lax.axis_index("leaf")
    col = lax.axis_index("cols")
    rows = bases.shape[1]
    width = right.shape[1]
    pair = 128 // panel_rank
    share = old_ref.shape[0]
    rank = bases.shape[2]
    line = n // 4
    z = me // 4
    low = me % 4
    stride_a = 1 + col % 2
    stride_b = 3 - stride_a
    near_a = me + stride_a * (1 - 2 * ((low // stride_a) % 2))
    near_b = me + stride_b * (1 - 2 * ((low // stride_b) % 2))
    near_ab = near_a + near_b - me
    third = rows // 3 // 16 * 16
    pieces = ((0, third), (third, third), (2 * third, rows - 2 * third))
    early = (0, 1)
    late = 2

    loads = [
        pltpu.make_async_copy(rows_hbm, bases.at[me], load_sem.at[0]),
        pltpu.make_async_copy(right_hbm, right, load_sem.at[1]),
    ]
    for load in loads:
        load.start()

    def left_load(index):
        span = pl.ds(pl.multiple_of(index * 128, 128), 128)
        return pltpu.make_async_copy(left_hbm.at[:, span], left.at[index], load_sem.at[2 + index])

    @pl.loop(0, width // 128)
    def _(index):
        left_load(index).start()

    barrier = pltpu.get_barrier_semaphore()

    @pl.loop(1, n)
    def _(step):
        pl.semaphore_signal(
            barrier, inc=1, device_id={"leaf": (me + step) % n}, device_id_type=MESH
        )

    for step in range(1, n_cols):
        pl.semaphore_signal(
            barrier, inc=1, device_id={"cols": (col + step) % n_cols}, device_id_type=MESH
        )
    pl.semaphore_wait(barrier, n - 1 + n_cols - 1)

    def hop(block, piece, way):
        start, size = pieces[piece]
        view = bases.at[block, pl.ds(start, size)]
        target = (near_a, near_b, me + 4, me - 4)[way]
        return pltpu.make_async_remote_copy(
            src_ref=view, dst_ref=view,
            send_sem=hop_send.at[way, block, piece], recv_sem=hop_recv.at[block, piece],
            device_id={"leaf": target}, device_id_type=MESH,
        )

    def go(block, piece, way):
        hop(block, piece, way).start()

    def gone(block, piece, way):
        hop(block, piece, way).wait_send()

    def arrived(block, piece):
        hop(block, piece, 0).wait_recv()

    def along(act, block, piece, upward, downward):
        if upward:
            @pl.when(z < line - 1)
            def _():
                act(block, piece, 2)
        if downward:
            @pl.when(z > 0)
            def _():
                act(block, piece, 3)

    def own_sends(act):
        for piece in range(3):
            along(act, me, piece, True, True)
            act(me, piece, 0)
            act(me, piece, 1)

    def first_sends(act, wait):
        for piece in early:
            if wait:
                arrived(near_a, piece)
            along(act, near_a, piece, True, True)
            act(near_a, piece, 1)
        if wait:
            arrived(near_a, late)
        act(near_a, late, 1)

    def sides(k, act):
        @pl.when(z - k >= 0)
        def _():
            act(-4 * k, True)

        @pl.when(z + k <= line - 1)
        def _():
            act(4 * k, False)

    def line_sends(k, act, wait):
        def same(shift, upward):
            for piece in early:
                for block in (me + shift, near_a + shift):
                    if wait:
                        arrived(block, piece)
                    along(act, block, piece, upward, not upward)
                    act(block, piece, 1)
            if wait:
                arrived(me + shift, late)
            along(act, me + shift, late, upward, not upward)
            act(me + shift, late, 0)
            act(me + shift, late, 1)

        def across(shift, upward):
            if wait:
                arrived(near_a + shift, late)
            act(near_a + shift, late, 1)

        sides(k, same)
        sides(k, across)

    def core_copy(step, block):
        return pltpu.make_async_remote_copy(
            src_ref=cores.at[block], dst_ref=coresr.at[step - 1, block],
            send_sem=core_send.at[step - 1, block], recv_sem=core_recv.at[step - 1, block],
            device_id={"cols": (col + step) % n_cols}, device_id_type=MESH,
        )

    def coef_copy(step):
        peer = (col + step) % n_cols
        return pltpu.make_async_remote_copy(
            src_ref=coefp.at[peer], dst_ref=coefr.at[step - 1],
            send_sem=coef_send.at[step - 1], recv_sem=coef_recv.at[step - 1],
            device_id={"cols": peer}, device_id_type=MESH,
        )

    def project(block):
        for slot in range(CAP):
            item = block * CAP + slot
            whole = dot_t(left[pair_ref[item]], bases[block])
            value = whole[:panel_rank] * weight_ref[item * pair]
            for piece in range(1, pair):
                inside = whole[piece * panel_rank : (piece + 1) * panel_rank]
                value = value + inside * weight_ref[item * pair + piece]
            cores[block, pl.ds(slot * panel_rank, panel_rank)] = value
        for step in range(1, n_cols):
            core_copy(step, block).start()

    def coef_chunk(index):
        start = pl.multiple_of(index * CHUNK, CHUNK)
        value = dot_t(basis_ref[...], right[:, pl.ds(start, CHUNK)])
        coefp[:, :, pl.ds(start, CHUNK)] = value.reshape(n_cols, share, CHUNK)

    loads[0].wait()
    own_sends(go)
    loads[1].wait()
    chunks = width // CHUNK
    pl.loop(0, chunks // 2)(coef_chunk)
    first_sends(go, True)
    pl.loop(chunks // 2, chunks)(coef_chunk)
    for step in range(1, n_cols):
        coef_copy(step).start()

    @pl.loop(0, width // 128)
    def _(index):
        left_load(index).wait()

    @pl.loop(0, 2)
    def _(index):
        project(me + index * (near_a - me))

    def far(k):
        def one(shift, upward):
            @pl.loop(0, 2)
            def _(index):
                block = near_b + index * (near_ab - near_b) + shift
                for piece in range(3):
                    arrived(block, piece)
                project(block)

        return one

    @pl.loop(1, line)
    def _(k):
        line_sends(k, go, True)

        def near(shift, upward):
            @pl.loop(0, 2)
            def _(index):
                project(me + index * (near_a - me) + shift)

        sides(k, near)

        @pl.when(k == 1)
        def _():
            far(0)(0, True)

        @pl.when(k > 1)
        def _():
            sides(k - 1, far(k - 1))

    levels = transfers_ref.shape[0]
    paths[0] = transfers_ref[levels - 1, 0]
    paths[1] = transfers_ref[levels - 1, 1]
    for level in range(levels - 2, -1, -1):
        count = 2 ** (levels - level)

        @pl.loop(0, count)
        def _(index):
            node = count - 1 - index
            paths[node] = jnp.dot(
                transfers_ref[level, node % 2], paths[node // 2],
                precision=HIGHEST, preferred_element_type=jnp.float32,
            )

    for step in range(1, n_cols):
        coef_copy(step).wait_recv()

    @pl.loop(0, width // 128)
    def _(index):
        span = pl.ds(pl.multiple_of(index * 128, 128), 128)
        total = coefp[col, :, span]
        for step in range(1, n_cols):
            total = total + coefr[step - 1, :, span]
        flipped = total.T.astype(jnp.bfloat16)
        for piece in range(pair):
            coeft[index * pair + piece] = flipped[piece * panel_rank : (piece + 1) * panel_rank]

    sides(line - 1, far(line - 1))

    def part_copy(block):
        return pltpu.make_async_remote_copy(
            src_ref=parts.at[block], dst_ref=partsr.at[me],
            send_sem=part_send.at[block], recv_sem=part_recv.at[me],
            device_id={"leaf": block}, device_id_type=MESH,
        )

    def strip_copy(block):
        return pltpu.make_async_remote_copy(
            src_ref=strips.at[block], dst_ref=stripsr.at[me],
            send_sem=strip_send.at[block], recv_sem=strip_recv.at[me],
            device_id={"leaf": block}, device_id_type=MESH,
        )

    def combined(block):
        for step in range(1, n_cols):
            core_copy(step, block).wait_recv()
        total = cores[block]
        for step in range(1, n_cols):
            total = total + coresr[step - 1, block]
        high = total.astype(jnp.bfloat16)
        low_part = (total - high.astype(jnp.float32)).astype(jnp.bfloat16)
        part = jnp.zeros((share, rank), jnp.float32)
        for slot in range(CAP):
            coef = coeft[source_ref[block * CAP + slot]]
            span = slice(slot * panel_rank, (slot + 1) * panel_rank)
            part = part + dot_t(coef, high[span]) + dot_t(coef, low_part[span])
        return part

    def add_root(block, part, total):
        return total + jnp.dot(
            part, paths[block], precision=HIGHEST, preferred_element_type=jnp.float32
        )

    def others(step, total):
        block = (me + step) % n
        part = combined(block)
        parts[block] = part.astype(jnp.bfloat16)
        part_copy(block).start()
        return add_root(block, part, total)

    root = lax.fori_loop(1, n, others, jnp.zeros((share, rank), jnp.float32))
    mine = combined(me) + old_ref[...]
    root = add_root(me, mine, root).T
    strip = rank // n
    for block in range(n):
        strips[block, :strip, :share] = root[block * strip : (block + 1) * strip]

    @pl.loop(1, n)
    def _(step):
        strip_copy((me + step) % n).start()

    def arrived_from(source):
        return pltpu.make_async_remote_copy(
            src_ref=parts.at[source], dst_ref=partsr.at[source],
            send_sem=part_send.at[source], recv_sem=part_recv.at[source],
            device_id={"leaf": source}, device_id_type=MESH,
        )

    def strip_from(source):
        return pltpu.make_async_remote_copy(
            src_ref=strips.at[source], dst_ref=stripsr.at[source],
            send_sem=strip_send.at[source], recv_sem=strip_recv.at[source],
            device_id={"leaf": source}, device_id_type=MESH,
        )

    leaf_ref[...] = mine

    @pl.loop(1, n)
    def _(step):
        source = (me + n - step) % n
        arrived_from(source).wait_recv()
        leaf_ref[...] += partsr[source].astype(jnp.float32)

    root_ref[...] = strips[me]

    @pl.loop(1, n)
    def _(step):
        source = (me + n - step) % n
        strip_from(source).wait_recv()
        root_ref[...] += stripsr[source]

    own_sends(gone)
    first_sends(gone, False)

    @pl.loop(1, line)
    def _(k):
        line_sends(k, gone, False)

    for step in range(1, n_cols):
        coef_copy(step).wait_send()

        @pl.loop(0, n)
        def _(block):
            core_copy(step, block).wait_send()

    @pl.loop(1, n)
    def _(step):
        part_copy((me + step) % n).wait_send()
        strip_copy((me + step) % n).wait_send()


def local(left_panels, right_panels, col_basis, row_bases, old_cores, transfers, targets):
    n = lax.axis_size("leaf")
    n_cols = lax.axis_size("cols")
    panels = targets.shape[0]
    rows, width = left_panels.shape
    panel_rank = width // panels
    rank = row_bases.shape[1]
    share = col_basis.shape[1] // n_cols
    strip = rank // n
    owners = targets[:, 0]
    order_ids = jnp.arange(panels, dtype=jnp.int32)
    same_owner = owners[:, None] == owners[None, :]
    earlier = order_ids[None, :] < order_ids[:, None]
    rank_in = jnp.sum(jnp.logical_and(same_owner, earlier).astype(jnp.int32), axis=1)
    matches = (owners * CAP + rank_in)[:, None] == jnp.arange(n * CAP, dtype=jnp.int32)[None, :]
    source = jnp.sum(jnp.where(matches, order_ids[:, None], 0), axis=0)
    pair = 128 // panel_rank
    inside = source[:, None] % pair == jnp.arange(pair, dtype=jnp.int32)[None, :]
    filled = jnp.any(matches, axis=0)[:, None]
    weights = jnp.logical_and(inside, filled).astype(jnp.float32).reshape(-1)
    old_share = lax.dynamic_slice_in_dim(old_cores[0], lax.axis_index("cols") * share, share, 0)

    vmem = pl.BlockSpec(memory_space=pltpu.VMEM)
    smem = pl.BlockSpec(memory_space=pltpu.SMEM)
    hbm = pl.BlockSpec(memory_space=pl.ANY)
    dma = pltpu.SemaphoreType.DMA
    bf16, f32 = jnp.bfloat16, jnp.float32
    leaf, root = pl.pallas_call(
        functools.partial(kernel, n, n_cols, panel_rank),
        out_shape=(
            jax.ShapeDtypeStruct((share, rank), f32),
            jax.ShapeDtypeStruct((8, 128), f32),
        ),
        in_specs=[smem, smem, smem, hbm, hbm, vmem, hbm, vmem, vmem],
        out_specs=(vmem, vmem),
        scratch_shapes=[
            pltpu.VMEM((width // 128, rows, 128), bf16),
            pltpu.VMEM((rows, width), bf16),
            pltpu.VMEM((n, rows, rank), bf16),
            pltpu.VMEM((n_cols, share, width), f32),
            pltpu.VMEM((n_cols - 1, share, width), f32),
            pltpu.VMEM((panels, panel_rank, share), bf16),
            pltpu.VMEM((n, CAP * panel_rank, rank), f32),
            pltpu.VMEM((n_cols - 1, n, CAP * panel_rank, rank), f32),
            pltpu.VMEM((n, rank, rank), f32),
            pltpu.VMEM((n, share, rank), bf16),
            pltpu.VMEM((n, share, rank), bf16),
            pltpu.VMEM((n, 8, 128), f32),
            pltpu.VMEM((n, 8, 128), f32),
            dma((2 + width // 128,)),
            dma((4, n, 3)),
            dma((n, 3)),
            dma((n_cols - 1,)),
            dma((n_cols - 1,)),
            dma((n_cols - 1, n)),
            dma((n_cols - 1, n)),
            dma((n,)),
            dma((n,)),
            dma((n,)),
            dma((n,)),
        ],
        compiler_params=pltpu.CompilerParams(
            collective_id=0, has_side_effects=True, vmem_limit_bytes=56 << 20
        ),
    )(source, source // pair, weights, left_panels, right_panels, col_basis, row_bases, old_share, transfers)
    return leaf[None], root[:strip, :share].T


def solution(mesh):
    placed = (
        P("cols", "leaf"),
        P("cols", "leaf"),
        P("cols", None),
        P("cols", "leaf"),
        P("leaf", None, None),
        P(),
        P("leaf", None),
    )
    return jax.shard_map(
        local,
        mesh=mesh,
        in_specs=placed,
        out_specs=(P("leaf", "cols", None), P("cols", "leaf")),
        check_vma=False,
    )
```

```python
import functools

import jax
import jax.numpy as jnp
from jax import lax
from jax.experimental import pallas as pl
from jax.experimental.pallas import tpu as pltpu
from jax.sharding import PartitionSpec as P

CAP = 2
HIGHEST = lax.Precision.HIGHEST
MESH = pl.DeviceIdType.MESH
CHUNK = 256
COUNT = 3
LATE = 1


def dot_t(lhs, rhs):
    return lax.dot_general(
        lhs, rhs, (((0,), (0,)), ((), ())), preferred_element_type=jnp.float32
    )


def kernel(
    n, n_cols, panel_rank,
    source_ref, pair_ref, weight_ref, left_hbm, right_hbm, basis_ref, rows_hbm, old_ref, transfers_ref,
    leaf_ref, root_ref,
    left, right, bases, coefp, coefr, coeft, cores, coresr, paths, parts, partsr, strips, stripsr,
    load_sem, hop_send, hop_recv, coef_send, coef_recv, core_send, core_recv,
    part_send, part_recv, strip_send, strip_recv,
):
    me = lax.axis_index("leaf")
    col = lax.axis_index("cols")
    rows = bases.shape[1]
    width = right.shape[1]
    pair = 128 // panel_rank
    share = old_ref.shape[0]
    rank = bases.shape[2]
    line = n // 4
    z = me // 4
    low = me % 4
    stride_a = 1 + col % 2
    stride_b = 3 - stride_a
    near_a = me + stride_a * (1 - 2 * ((low // stride_a) % 2))
    near_b = me + stride_b * (1 - 2 * ((low // stride_b) % 2))
    near_ab = near_a + near_b - me
    size = rows // COUNT // 16 * 16
    pieces = [(index * size, size) for index in range(COUNT - 1)]
    pieces.append(((COUNT - 1) * size, rows - (COUNT - 1) * size))
    late = range(LATE)
    early = range(LATE, COUNT)

    loads = [
        pltpu.make_async_copy(rows_hbm, bases.at[me], load_sem.at[0]),
        pltpu.make_async_copy(right_hbm, right, load_sem.at[1]),
    ]
    for load in loads:
        load.start()

    def left_load(index):
        span = pl.ds(pl.multiple_of(index * 128, 128), 128)
        return pltpu.make_async_copy(left_hbm.at[:, span], left.at[index], load_sem.at[2 + index])

    @pl.loop(0, width // 128)
    def _(index):
        left_load(index).start()

    barrier = pltpu.get_barrier_semaphore()

    @pl.loop(1, n)
    def _(step):
        pl.semaphore_signal(
            barrier, inc=1, device_id={"leaf": (me + step) % n}, device_id_type=MESH
        )

    for step in range(1, n_cols):
        pl.semaphore_signal(
            barrier, inc=1, device_id={"cols": (col + step) % n_cols}, device_id_type=MESH
        )
    pl.semaphore_wait(barrier, n - 1 + n_cols - 1)

    def hop(block, piece, way):
        start, size = pieces[piece]
        view = bases.at[block, pl.ds(start, size)]
        target = (near_a, near_b, me + 4, me - 4)[way]
        return pltpu.make_async_remote_copy(
            src_ref=view, dst_ref=view,
            send_sem=hop_send.at[way, block, piece], recv_sem=hop_recv.at[block, piece],
            device_id={"leaf": target}, device_id_type=MESH,
        )

    def go(block, piece, way):
        hop(block, piece, way).start()

    def gone(block, piece, way):
        hop(block, piece, way).wait_send()

    def arrived(block, piece):
        hop(block, piece, 0).wait_recv()

    def along(act, block, piece, upward, downward):
        if upward:
            @pl.when(z < line - 1)
            def _():
                act(block, piece, 2)
        if downward:
            @pl.when(z > 0)
            def _():
                act(block, piece, 3)

    def own_sends(act):
        for piece in early:
            act(me, piece, 0)
        for piece in range(COUNT):
            along(act, me, piece, True, True)
        for piece in late:
            act(me, piece, 0)

    def own_last(act):
        for piece in range(COUNT):
            act(me, piece, 1)

    def first_sends(act, wait):
        for piece in early:
            if wait:
                arrived(near_a, piece)
            along(act, near_a, piece, True, True)
        own_last(act)
        for piece in early:
            act(near_a, piece, 1)
        for piece in late:
            if wait:
                arrived(near_a, piece)
            act(near_a, piece, 1)

    def sides(k, act):
        @pl.when(z - k >= 0)
        def _():
            act(-4 * k, True)

        @pl.when(z + k <= line - 1)
        def _():
            act(4 * k, False)

    def line_sends(k, act, wait):
        def same(shift, upward):
            for piece in late:
                if wait:
                    arrived(me + shift, piece)
                along(act, me + shift, piece, upward, not upward)
                act(me + shift, piece, 0)
                act(me + shift, piece, 1)
            for block in (me + shift, near_a + shift):
                for piece in early:
                    if wait:
                        arrived(block, piece)
                    along(act, block, piece, upward, not upward)
                    act(block, piece, 1)

        def across(shift, upward):
            for piece in late:
                if wait:
                    arrived(near_a + shift, piece)
                act(near_a + shift, piece, 1)

        sides(k, same)
        sides(k, across)

    def core_copy(step, block):
        return pltpu.make_async_remote_copy(
            src_ref=cores.at[block], dst_ref=coresr.at[step - 1, block],
            send_sem=core_send.at[step - 1, block], recv_sem=core_recv.at[step - 1, block],
            device_id={"cols": (col + step) % n_cols}, device_id_type=MESH,
        )

    def coef_copy(step):
        peer = (col + step) % n_cols
        return pltpu.make_async_remote_copy(
            src_ref=coefp.at[peer], dst_ref=coefr.at[step - 1],
            send_sem=coef_send.at[step - 1], recv_sem=coef_recv.at[step - 1],
            device_id={"cols": peer}, device_id_type=MESH,
        )

    def project(block):
        for slot in range(CAP):
            item = block * CAP + slot
            whole = dot_t(left[pair_ref[item]], bases[block])
            value = whole[:panel_rank] * weight_ref[item * pair]
            for piece in range(1, pair):
                inside = whole[piece * panel_rank : (piece + 1) * panel_rank]
                value = value + inside * weight_ref[item * pair + piece]
            cores[block, pl.ds(slot * panel_rank, panel_rank)] = value
        for step in range(1, n_cols):
            core_copy(step, block).start()

    def coef_chunk(index):
        start = pl.multiple_of(index * CHUNK, CHUNK)
        value = dot_t(basis_ref[...], right[:, pl.ds(start, CHUNK)])
        coefp[:, :, pl.ds(start, CHUNK)] = value.reshape(n_cols, share, CHUNK)

    loads[0].wait()
    own_sends(go)
    first_sends(go, True)
    loads[1].wait()
    chunks = width // CHUNK
    pl.loop(0, chunks)(coef_chunk)
    for step in range(1, n_cols):
        coef_copy(step).start()

    @pl.loop(0, width // 128)
    def _(index):
        left_load(index).wait()

    @pl.loop(0, 2)
    def _(index):
        project(me + index * (near_a - me))

    def far(k):
        def one(shift, upward):
            @pl.loop(0, 2)
            def _(index):
                block = near_b + index * (near_ab - near_b) + shift
                for piece in range(COUNT):
                    arrived(block, piece)
                project(block)

        return one

    @pl.loop(1, line)
    def _(k):
        line_sends(k, go, True)

        def near(shift, upward):
            @pl.loop(0, 2)
            def _(index):
                project(me + index * (near_a - me) + shift)

        sides(k, near)

        @pl.when(k == 1)
        def _():
            far(0)(0, True)

        @pl.when(k > 1)
        def _():
            sides(k - 1, far(k - 1))

    levels = transfers_ref.shape[0]
    paths[0] = transfers_ref[levels - 1, 0]
    paths[1] = transfers_ref[levels - 1, 1]
    for level in range(levels - 2, -1, -1):
        count = 2 ** (levels - level)

        @pl.loop(0, count)
        def _(index):
            node = count - 1 - index
            paths[node] = jnp.dot(
                transfers_ref[level, node % 2], paths[node // 2],
                precision=HIGHEST, preferred_element_type=jnp.float32,
            )

    for step in range(1, n_cols):
        coef_copy(step).wait_recv()

    @pl.loop(0, width // 128)
    def _(index):
        span = pl.ds(pl.multiple_of(index * 128, 128), 128)
        total = coefp[col, :, span]
        for step in range(1, n_cols):
            total = total + coefr[step - 1, :, span]
        flipped = total.T.astype(jnp.bfloat16)
        for piece in range(pair):
            coeft[index * pair + piece] = flipped[piece * panel_rank : (piece + 1) * panel_rank]

    sides(line - 1, far(line - 1))

    def part_copy(block):
        return pltpu.make_async_remote_copy(
            src_ref=parts.at[block], dst_ref=partsr.at[me],
            send_sem=part_send.at[block], recv_sem=part_recv.at[me],
            device_id={"leaf": block}, device_id_type=MESH,
        )

    def strip_copy(block):
        return pltpu.make_async_remote_copy(
            src_ref=strips.at[block], dst_ref=stripsr.at[me],
            send_sem=strip_send.at[block], recv_sem=strip_recv.at[me],
            device_id={"leaf": block}, device_id_type=MESH,
        )

    def combined(block):
        for step in range(1, n_cols):
            core_copy(step, block).wait_recv()
        total = cores[block]
        for step in range(1, n_cols):
            total = total + coresr[step - 1, block]
        high = total.astype(jnp.bfloat16)
        low_part = (total - high.astype(jnp.float32)).astype(jnp.bfloat16)
        part = jnp.zeros((share, rank), jnp.float32)
        for slot in range(CAP):
            coef = coeft[source_ref[block * CAP + slot]]
            span = slice(slot * panel_rank, (slot + 1) * panel_rank)
            part = part + dot_t(coef, high[span]) + dot_t(coef, low_part[span])
        return part

    def add_root(block, part, total):
        return total + jnp.dot(
            part, paths[block], precision=HIGHEST, preferred_element_type=jnp.float32
        )

    def others(step, total):
        block = (me + step) % n
        part = combined(block)
        parts[block] = part.astype(jnp.bfloat16)
        part_copy(block).start()
        return add_root(block, part, total)

    root = lax.fori_loop(1, n, others, jnp.zeros((share, rank), jnp.float32))
    mine = combined(me) + old_ref[...]
    root = add_root(me, mine, root).T
    strip = rank // n
    for block in range(n):
        strips[block, :strip, :share] = root[block * strip : (block + 1) * strip]

    @pl.loop(1, n)
    def _(step):
        strip_copy((me + step) % n).start()

    def arrived_from(source):
        return pltpu.make_async_remote_copy(
            src_ref=parts.at[source], dst_ref=partsr.at[source],
            send_sem=part_send.at[source], recv_sem=part_recv.at[source],
            device_id={"leaf": source}, device_id_type=MESH,
        )

    def strip_from(source):
        return pltpu.make_async_remote_copy(
            src_ref=strips.at[source], dst_ref=stripsr.at[source],
            send_sem=strip_send.at[source], recv_sem=strip_recv.at[source],
            device_id={"leaf": source}, device_id_type=MESH,
        )

    leaf_ref[...] = mine

    @pl.loop(1, n)
    def _(step):
        source = (me + n - step) % n
        arrived_from(source).wait_recv()
        leaf_ref[...] += partsr[source].astype(jnp.float32)

    root_ref[...] = strips[me]

    @pl.loop(1, n)
    def _(step):
        source = (me + n - step) % n
        strip_from(source).wait_recv()
        root_ref[...] += stripsr[source]

    own_sends(gone)
    first_sends(gone, False)

    @pl.loop(1, line)
    def _(k):
        line_sends(k, gone, False)

    for step in range(1, n_cols):
        coef_copy(step).wait_send()

        @pl.loop(0, n)
        def _(block):
            core_copy(step, block).wait_send()

    @pl.loop(1, n)
    def _(step):
        part_copy((me + step) % n).wait_send()
        strip_copy((me + step) % n).wait_send()


def local(left_panels, right_panels, col_basis, row_bases, old_cores, transfers, targets):
    n = lax.axis_size("leaf")
    n_cols = lax.axis_size("cols")
    panels = targets.shape[0]
    rows, width = left_panels.shape
    panel_rank = width // panels
    rank = row_bases.shape[1]
    share = col_basis.shape[1] // n_cols
    strip = rank // n
    owners = targets[:, 0]
    order_ids = jnp.arange(panels, dtype=jnp.int32)
    same_owner = owners[:, None] == owners[None, :]
    earlier = order_ids[None, :] < order_ids[:, None]
    rank_in = jnp.sum(jnp.logical_and(same_owner, earlier).astype(jnp.int32), axis=1)
    matches = (owners * CAP + rank_in)[:, None] == jnp.arange(n * CAP, dtype=jnp.int32)[None, :]
    source = jnp.sum(jnp.where(matches, order_ids[:, None], 0), axis=0)
    pair = 128 // panel_rank
    inside = source[:, None] % pair == jnp.arange(pair, dtype=jnp.int32)[None, :]
    filled = jnp.any(matches, axis=0)[:, None]
    weights = jnp.logical_and(inside, filled).astype(jnp.float32).reshape(-1)
    old_share = lax.dynamic_slice_in_dim(old_cores[0], lax.axis_index("cols") * share, share, 0)

    vmem = pl.BlockSpec(memory_space=pltpu.VMEM)
    smem = pl.BlockSpec(memory_space=pltpu.SMEM)
    hbm = pl.BlockSpec(memory_space=pl.ANY)
    dma = pltpu.SemaphoreType.DMA
    bf16, f32 = jnp.bfloat16, jnp.float32
    leaf, root = pl.pallas_call(
        functools.partial(kernel, n, n_cols, panel_rank),
        out_shape=(
            jax.ShapeDtypeStruct((share, rank), f32),
            jax.ShapeDtypeStruct((8, 128), f32),
        ),
        in_specs=[smem, smem, smem, hbm, hbm, vmem, hbm, vmem, vmem],
        out_specs=(vmem, vmem),
        scratch_shapes=[
            pltpu.VMEM((width // 128, rows, 128), bf16),
            pltpu.VMEM((rows, width), bf16),
            pltpu.VMEM((n, rows, rank), bf16),
            pltpu.VMEM((n_cols, share, width), f32),
            pltpu.VMEM((n_cols - 1, share, width), f32),
            pltpu.VMEM((panels, panel_rank, share), bf16),
            pltpu.VMEM((n, CAP * panel_rank, rank), f32),
            pltpu.VMEM((n_cols - 1, n, CAP * panel_rank, rank), f32),
            pltpu.VMEM((n, rank, rank), f32),
            pltpu.VMEM((n, share, rank), bf16),
            pltpu.VMEM((n, share, rank), bf16),
            pltpu.VMEM((n, 8, 128), f32),
            pltpu.VMEM((n, 8, 128), f32),
            dma((2 + width // 128,)),
            dma((4, n, COUNT)),
            dma((n, COUNT)),
            dma((n_cols - 1,)),
            dma((n_cols - 1,)),
            dma((n_cols - 1, n)),
            dma((n_cols - 1, n)),
            dma((n,)),
            dma((n,)),
            dma((n,)),
            dma((n,)),
        ],
        compiler_params=pltpu.CompilerParams(
            collective_id=0, has_side_effects=True, vmem_limit_bytes=56 << 20
        ),
    )(source, source // pair, weights, left_panels, right_panels, col_basis, row_bases, old_share, transfers)
    return leaf[None], root[:strip, :share].T


def solution(mesh):
    placed = (
        P("cols", "leaf"),
        P("cols", "leaf"),
        P("cols", None),
        P("cols", "leaf"),
        P("leaf", None, None),
        P(),
        P("leaf", None),
    )
    return jax.shard_map(
        local,
        mesh=mesh,
        in_specs=placed,
        out_specs=(P("leaf", "cols", None), P("cols", "leaf")),
        check_vma=False,
    )
```
